32 devices in a mesh: survey: 2 (over x), depth: 16 (over z, y, core).
Axes of the slice: x: 2, y: 2, z: 4, core: 2. Of those that a mesh axis runs over, the one named last changes fastest.
Arguments:
- arriving: float32 [32, 2, 2, 4, 128, 128], P(('survey', 'depth')), parts along dimension 0, may hold values from -3.1 to 3.1
- classes: int32 [16, 128, 128], P('depth'), may hold values from 0 to 15
- filters: float32 [18, 4, 2, 6, 16], replicated, may hold values from -1.25 to 1.25
- src_pos: int32 [4, 4, 2], P('survey'), parts along dimension 0, may hold values from 0 to 127
- wavelet: float32 [4, 4, 2, 4], P('survey'), parts along dimension 0, may hold values from -6 to 6
- rec_pos: int32 [1024, 2], P('survey'), parts along dimension 0, may hold values from 0 to 127
- rec_data: float32 [4, 2, 4, 512], P('survey'), parts along dimension 0, may hold values from -6 to 6
Outputs:
- image: float32 [32, 128, 128], P(('survey', 'depth')), parts along dimension 0
- passing: float32 [32, 2, 2, 4, 128, 128], P(('survey', 'depth')), parts along dimension 0
The draws below stay inside these ranges and needn't reach their ends.
There are 2 independent parts, one for each index of `survey`. The reference program is written for one: setup_inputs(seed, part) draws one part's arguments, and reference() takes and returns one part's arrays. A program takes and returns all parts, laid end to end along the dimension named above; an argument that names none is the same for every part. Nothing has to cross between parts.
All inputs are finite; a program needn't handle non-finite values.
Results may differ from the reference program's by a relative error of at most 0.0001.
Values sent between devices are 32-bit elements; how exact they have to be, the bound alone decides.
A program may use at most 64 MiB of HBM per device.

```python
import math
import jax
import jax.numpy as jnp
from jax import lax

LAT = 128
NF = 4
NREC = 512
TICKS = 3
TERMS = 6
CLASSES = 16
SOURCES = 4
SLABS = 16
NZ = 16
BLOCKS = 18
NEW = 2


def draw_arriving(key, part):
    extent = (SLABS, 2, 2, NF, LAT, LAT)
    slab_axis = jnp.arange(SLABS, dtype=jnp.float32)
    growth = jnp.exp(math.log(3.0) * slab_axis / max(SLABS - 1, 1))
    values = jax.random.truncated_normal(key, -4.0, 4.0, extent, jnp.float32)
    return (0.05 * values * growth.reshape(SLABS, 1, 1, 1, 1, 1)).astype(jnp.float32)


def draw_filters(key, part):
    argument = jax.random.uniform(key, (BLOCKS, NF, 1, 1, CLASSES), jnp.float32, 0.3, 1.6)
    half_arg = 0.5 * argument
    term_list = []
    for term_index in range(TERMS):
        running = jnp.zeros_like(half_arg)
        for series_index in range(12):
            factor = (-1.0) ** series_index / (math.factorial(series_index) * math.factorial(series_index + term_index))
            running = running + factor * half_arg ** (2 * series_index + term_index)
        weight = 1.0 if term_index == 0 else 2.0
        phases = [(1.0, 0.0), (0.0, 1.0), (-1.0, 0.0), (0.0, -1.0)][term_index % 4]
        term_list.append(jnp.concatenate([phases[0] * weight * running, phases[1] * weight * running], axis=2))
    return (0.97 * jnp.concatenate(term_list, axis=3)).astype(jnp.float32)


def set_ends(values, key, smallest, high):
    place = [jax.random.randint(jax.random.fold_in(key, axis), (), 0, length) for axis, length in enumerate(values.shape)]
    main_axis = values.shape.index(max(values.shape))
    neighbour = place[:main_axis] + [(place[main_axis] + 1) % values.shape[main_axis]] + place[main_axis + 1:]
    return values.at[tuple(place)].set(smallest).at[tuple(neighbour)].set(high)


def normal_values(key, dims, deviation, most, held_as=jnp.bfloat16):
    result = jax.random.normal(key, dims, jnp.float32) * deviation
    return jnp.minimum(jnp.maximum(result, -most), most).astype(held_as)


def setup_inputs(seed: int = 0, part: int = 0) -> dict:
    key_list = jax.random.split(jax.random.key(seed), 8)
    part_splits = jax.random.split(jax.random.fold_in(key_list[7], part), 8)
    return {
        "arriving": draw_arriving(jax.random.fold_in(jax.random.fold_in(key_list[7], part), 71), part),
        "classes": set_ends(jax.random.randint(key_list[1], (NZ, LAT, LAT), 0, CLASSES), jax.random.fold_in(key_list[1], 1), 0, CLASSES - 1).astype(jnp.int32),
        "filters": draw_filters(jax.random.fold_in(key_list[7], 71), part),
        "src_pos": set_ends(jax.random.randint(part_splits[3], (NEW, SOURCES, 2), 0, LAT), jax.random.fold_in(part_splits[3], 1), 0, LAT - 1).astype(jnp.int32),
        "wavelet": normal_values(part_splits[4], (NEW, SOURCES, 2, NF), 1.0, 6.0, jnp.float32),
        "rec_pos": set_ends(jax.random.randint(part_splits[5], (NREC, 2), 0, LAT), jax.random.fold_in(part_splits[5], 1), 0, LAT - 1).astype(jnp.int32),
        "rec_data": normal_values(part_splits[6], (NEW, 2, NF, NREC), 1.0, 6.0, jnp.float32),
    }


def lateral(wavefield):
    padded = jnp.pad(wavefield, ((0, 0), (0, 0), (1, 1), (0, 0)))
    across = 0.25 * padded[:, :, :-2, :] + 0.5 * wavefield + 0.25 * padded[:, :, 2:, :]
    padded = jnp.pad(across, ((0, 0), (0, 0), (0, 0), (1, 1)))
    smooth = 0.25 * padded[:, :, :, :-2] + 0.5 * across + 0.25 * padded[:, :, :, 2:]
    return 2.0 * smooth - wavefield

def extrapolate(wavefield, coefficients, conjugate):
    real_part = coefficients[:, 0]
    imag_part = conjugate * coefficients[:, 1]
    previous = wavefield
    current = lateral(wavefield)
    real_sum = real_part[:, 0] * previous[0] - imag_part[:, 0] * previous[1] + real_part[:, 1] * current[0] - imag_part[:, 1] * current[1]
    imag_sum = real_part[:, 0] * previous[1] + imag_part[:, 0] * previous[0] + real_part[:, 1] * current[1] + imag_part[:, 1] * current[0]
    for term_index in range(2, coefficients.shape[2]):
        following = 2.0 * lateral(current) - previous
        real_sum = real_sum + real_part[:, term_index] * following[0] - imag_part[:, term_index] * following[1]
        imag_sum = imag_sum + real_part[:, term_index] * following[1] + imag_part[:, term_index] * following[0]
        previous, current = (current, following)
    return jnp.stack([real_sum, imag_sum])

def pick_rows(table_rows, labels_grid):
    return table_rows[..., labels_grid]

def inject(src_pos, wavelet, rec_pos, rec_data, tick_index):
    source = jnp.zeros((2, NF, LAT, LAT), jnp.float32)
    for emitter in range(SOURCES):
        source = source.at[:, :, src_pos[tick_index, emitter, 0], src_pos[tick_index, emitter, 1]].add(wavelet[tick_index, emitter])
    receiver = jnp.zeros((2, NF, LAT, LAT), jnp.float32)
    receiver = receiver.at[:, :, rec_pos[:, 0], rec_pos[:, 1]].add(rec_data[tick_index])
    return jnp.stack([source, receiver])

def reference(arriving, classes, filters, src_pos, wavelet, rec_pos, rec_data):
    levels = classes.shape[0] // SLABS
    labels_all = classes.reshape(SLABS, levels, LAT, LAT)
    fields = arriving
    correlation = jnp.zeros((SLABS, levels, LAT, LAT), jnp.float32)
    illumination = jnp.zeros((SLABS, levels, LAT, LAT), jnp.float32)
    for tick_index in range(TICKS):
        block_ids = (tick_index - jnp.arange(SLABS, dtype=jnp.int32) + SLABS - 1).astype(jnp.int32)
        table_all = filters[block_ids]
        for depth_row in range(levels):
            coefficients = jax.vmap(pick_rows)(table_all, labels_all[:, depth_row])
            source = fields[:, 0]
            receiver = fields[:, 1]
            correlation = correlation.at[:, depth_row].add(lax.optimization_barrier(jnp.sum(source[:, 0] * receiver[:, 0] + source[:, 1] * receiver[:, 1], axis=1)))
            illumination = illumination.at[:, depth_row].add(lax.optimization_barrier(jnp.sum(source[:, 0] * source[:, 0] + source[:, 1] * source[:, 1], axis=1)))
            source = jax.vmap(extrapolate, in_axes=(0, 0, None))(source, coefficients, 1.0)
            receiver = jax.vmap(extrapolate, in_axes=(0, 0, None))(receiver, coefficients, -1.0)
            fields = jnp.stack([source, receiver], axis=1)
        if tick_index + 1 < TICKS:
            fields = jnp.concatenate([inject(src_pos, wavelet, rec_pos, rec_data, tick_index)[None], fields[:-1]], axis=0)
    damping = jnp.sum(illumination) / (SLABS * levels * LAT * LAT)
    image = math.sqrt(TICKS * NF) * correlation / (illumination + damping)
    return (image.reshape(SLABS * levels, LAT, LAT), fields)
```

```python
import functools
import math

import jax
import jax.numpy as jnp
from jax import lax
from jax.experimental import pallas as pl
from jax.experimental.pallas import tpu as pltpu
from jax.sharding import PartitionSpec as P

MESH = pl.DeviceIdType.MESH
PAD = 8


def kernel(
    chain,
    ticks,
    freqs,
    terms,
    width,
    src_pos,
    wavelet,
    arriving,
    classes,
    filters,
    rec_pos,
    rec_data,
    image,
    passing,
    fields,
    leaving,
    table,
    coef,
    terms_buf,
    corr,
    illum,
    totals,
    rec_x,
    rec_y,
    in_sem,
    table_sem,
    out_sem,
    send_sem,
    recv_sem,
    tot_send,
    tot_recv,
):
    position = lax.axis_index("depth")
    has_next = position < chain - 1
    following_slab = lax.rem(position + 1, chain)
    is_first = position == 0

    def load_copy(kind, freq):
        return pltpu.make_async_copy(
            arriving.at[0, kind, :, freq], fields.at[0, kind, :, freq], in_sem.at[kind, freq]
        )

    def send_copy(tick, kind, freq):
        return pltpu.make_async_remote_copy(
            src_ref=leaving.at[tick, kind, :, freq],
            dst_ref=fields.at[tick + 1, kind, :, freq],
            send_sem=send_sem.at[tick, kind, freq],
            recv_sem=recv_sem.at[tick, kind, freq],
            device_id={"depth": following_slab},
            device_id_type=MESH,
        )

    def out_copy(kind, freq):
        return pltpu.make_async_copy(
            leaving.at[ticks - 1, kind, :, freq],
            passing.at[0, kind, :, freq],
            out_sem.at[kind, freq],
        )

    def total_copy(other):
        return pltpu.make_async_remote_copy(
            src_ref=totals.at[position],
            dst_ref=totals.at[position],
            send_sem=tot_send.at[other],
            recv_sem=tot_recv.at[position],
            device_id={"depth": other},
            device_id_type=MESH,
        )

    def total_arrival(other):
        return pltpu.make_async_remote_copy(
            src_ref=totals.at[other],
            dst_ref=totals.at[other],
            send_sem=tot_send.at[other],
            recv_sem=tot_recv.at[other],
            device_id={"depth": other},
            device_id_type=MESH,
        )

    table_copy = pltpu.make_async_copy(
        filters.at[pl.ds(chain - 1 - position, ticks)], table, table_sem
    )
    table_copy.start()
    for kind in range(2):
        for freq in range(freqs):
            load_copy(kind, freq).start()

    barrier = pltpu.get_barrier_semaphore()

    @pl.loop(1, chain)
    def _(step):
        pl.semaphore_signal(
            barrier,
            inc=1,
            device_id={"depth": lax.rem(position + step, chain)},
            device_id_type=MESH,
        )

    corr[...] = jnp.zeros_like(corr)
    illum[...] = jnp.zeros_like(illum)
    edge = jnp.zeros((2, terms, PAD, width), jnp.float32)
    terms_buf[:, :, 0:PAD, :] = edge
    terms_buf[:, :, PAD + width : 2 * PAD + width, :] = edge
    table_copy.wait()

    def gather_coefficients(tick, freq):
        cells = classes[0]
        for part in range(2):
            rows = table[tick, freq, part]
            rows = jnp.concatenate(
                [rows, jnp.zeros((terms, width - rows.shape[1]), jnp.float32)], axis=1
            )
            for term in range(terms):
                row = jnp.broadcast_to(rows[term : term + 1, :], (width, width))
                coef[freq, part, term] = jnp.take_along_axis(
                    row, cells, axis=1, mode="promise_in_bounds"
                )

    lane = lax.broadcasted_iota(jnp.int32, (width, width), 1)
    first_lane = lane == 0
    last_lane = lane == width - 1

    def smooth(part, term):
        centre = terms_buf[part, term, PAD : PAD + width, :]
        rows = (
            terms_buf[part, term, PAD - 1 : PAD - 1 + width, :]
            + terms_buf[part, term, PAD + 1 : PAD + 1 + width, :]
        ) + (centre + centre)
        left = jnp.where(first_lane, 0.0, pltpu.roll(rows, 1, 1))
        right = jnp.where(last_lane, 0.0, pltpu.roll(rows, width - 1, 1))
        return centre, (left + right) + (rows + rows)

    def depth_step(tick, kind, freq):
        sign = 1.0 if kind == 0 else -1.0
        for part in range(2):
            terms_buf[part, 0, PAD : PAD + width, :] = fields[tick, kind, part, freq]
        for term in range(1, terms):
            for part in range(2):
                centre, total = smooth(part, term - 1)
                if term == 1:
                    value = 0.125 * total - centre
                else:
                    previous = terms_buf[part, term - 2, PAD : PAD + width, :]
                    value = 0.25 * total - ((centre + centre) + previous)
                terms_buf[part, term, PAD : PAD + width, :] = value
        for tile in range(0, width, 16):
            cells = slice(tile, tile + 16)
            padded = slice(PAD + tile, PAD + tile + 16)
            real, imag = 0.0, 0.0
            for term in range(terms):
                c_real = coef[freq, 0, term, cells, :]
                c_imag = sign * coef[freq, 1, term, cells, :]
                q_real = terms_buf[0, term, padded, :]
                q_imag = terms_buf[1, term, padded, :]
                real = real + (c_real * q_real - c_imag * q_imag)
                imag = imag + (c_real * q_imag + c_imag * q_real)
            leaving[tick, kind, 0, freq, cells, :] = real
            leaving[tick, kind, 1, freq, cells, :] = imag

    def inject(tick):
        column = lax.broadcasted_iota(jnp.int32, rec_y.shape, 1)
        if tick == 0:
            hits_x = (rec_pos[:, 0:1] == column).astype(jnp.float32)
            rec_x[...] = jnp.transpose(hits_x)
            rec_y[...] = (rec_pos[:, 1:2] == column).astype(jnp.float32)
        grid_x = lax.broadcasted_iota(jnp.int32, (width, width), 0)
        grid_y = lax.broadcasted_iota(jnp.int32, (width, width), 1)
        hits = [
            (grid_x == src_pos[tick, e, 0]) & (grid_y == src_pos[tick, e, 1])
            for e in range(src_pos.shape[1])
        ]
        for part in range(2):
            for freq in range(freqs):
                plane = jnp.zeros((width, width), jnp.float32)
                for e, hit in enumerate(hits):
                    plane = plane + jnp.where(hit, wavelet[tick, e, part, freq], 0.0)
                fields[tick + 1, 0, part, freq] = plane
                weights = rec_data[tick, part, freq : freq + 1, :]
                fields[tick + 1, 1, part, freq] = jnp.dot(
                    rec_x[...] * weights,
                    rec_y[...],
                    precision=lax.Precision.HIGHEST,
                    preferred_element_type=jnp.float32,
                )

    for tick in range(ticks):
        if tick > 0:
            pl.when(is_first)(functools.partial(inject, tick - 1))
        for kind in range(2):

            def chunk(freq, carry, tick=tick, kind=kind):
                if kind == 0:
                    gather_coefficients(tick, freq)
                if tick == 0:
                    load_copy(kind, freq).wait()
                else:

                    @pl.when(position > 0)
                    def _():
                        send_copy(tick - 1, kind, freq).wait_recv()

                depth_step(tick, kind, freq)
                if tick == 0 and kind == 0:

                    @pl.when(freq == 0)
                    def _():
                        pl.semaphore_wait(barrier, chain - 1)

                if tick < ticks - 1:

                    @pl.when(has_next)
                    def _():
                        send_copy(tick, kind, freq).start()
                else:
                    out_copy(kind, freq).start()
                real = fields[tick, 0, 0, freq]
                imag = fields[tick, 0, 1, freq]
                if kind == 0:
                    illum[...] += real * real + imag * imag
                else:
                    corr[...] += real * fields[tick, 1, 0, freq] + imag * fields[tick, 1, 1, freq]
                return carry

            lax.fori_loop(0, freqs, chunk, 0)
            if tick == ticks - 1 and kind == 0:
                totals[position] = jnp.sum(illum[...].reshape(width // 8, 8, width), axis=0)

                @pl.loop(1, chain)
                def _(step):
                    total_copy(lax.rem(position + step, chain)).start()

    @pl.loop(1, chain)
    def _(step):
        total_arrival(lax.rem(position + step, chain)).wait_recv()

    energy = jnp.sum(jnp.sum(totals[...], axis=0), keepdims=True)
    damping = energy / (chain * width * width)
    image[0] = math.sqrt(ticks * freqs) * corr[...] / (illum[...] + damping)

    @pl.loop(1, chain)
    def _(step):
        total_copy(lax.rem(position + step, chain)).wait_send()

    for kind in range(2):
        for freq in range(freqs):
            for tick in range(ticks - 1):

                @pl.when(has_next)
                def _():
                    send_copy(tick, kind, freq).wait_send()

            out_copy(kind, freq).wait()


def solution(mesh):
    chain = mesh.shape["depth"]

    def body(arriving, classes, filters, src_pos, wavelet, rec_pos, rec_data):
        _, kinds, parts, freqs, width, _ = arriving.shape
        ticks = wavelet.shape[0] + 1
        terms, labels = filters.shape[3:]
        receivers = rec_pos.shape[0]
        f32 = jnp.float32
        vmem = pl.BlockSpec(memory_space=pltpu.VMEM)
        smem = pl.BlockSpec(memory_space=pltpu.SMEM)
        hbm = pl.BlockSpec(memory_space=pl.ANY)
        window = (ticks, kinds, parts, freqs, width, width)
        return pl.pallas_call(
            functools.partial(kernel, chain, ticks, freqs, terms, width),
            out_shape=(
                jax.ShapeDtypeStruct((1, width, width), f32),
                jax.ShapeDtypeStruct(arriving.shape, f32),
            ),
            in_specs=[smem, smem, hbm, vmem, hbm, vmem, vmem],
            out_specs=(vmem, hbm),
            scratch_shapes=[
                pltpu.VMEM(window, f32),
                pltpu.VMEM(window, f32),
                pltpu.VMEM((ticks, freqs, parts, terms, labels), f32),
                pltpu.VMEM((freqs, parts, terms, width, width), f32),
                pltpu.VMEM((parts, terms, width + 2 * PAD, width), f32),
                pltpu.VMEM((width, width), f32),
                pltpu.VMEM((width, width), f32),
                pltpu.VMEM((chain, 8, width), f32),
                pltpu.VMEM((width, receivers), f32),
                pltpu.VMEM((receivers, width), f32),
                pltpu.SemaphoreType.DMA((kinds, freqs)),
                pltpu.SemaphoreType.DMA,
                pltpu.SemaphoreType.DMA((kinds, freqs)),
                pltpu.SemaphoreType.DMA((ticks - 1, kinds, freqs)),
                pltpu.SemaphoreType.DMA((ticks - 1, kinds, freqs)),
                pltpu.SemaphoreType.DMA((chain,)),
                pltpu.SemaphoreType.DMA((chain,)),
            ],
            compiler_params=pltpu.CompilerParams(
                collective_id=0, has_side_effects=True, vmem_limit_bytes=40 << 20
            ),
        )(src_pos, wavelet, arriving, classes, filters, rec_pos, rec_data)

    return jax.shard_map(
        body,
        mesh=mesh,
        in_specs=(
            P(("survey", "depth"), None, None, None, None, None),
            P("depth", None, None),
            P(),
            P("survey", None, None),
            P("survey", None, None, None),
            P("survey", None),
            P("survey", None, None, None),
        ),
        out_specs=(
            P(("survey", "depth"), None, None),
            P(("survey", "depth"), None, None, None, None, None),
        ),
        check_vma=False,
    )
```

```python
import functools
import math

import jax
import jax.numpy as jnp
from jax import lax
from jax.experimental import pallas as pl
from jax.experimental.pallas import tpu as pltpu
from jax.sharding import PartitionSpec as P

MESH = pl.DeviceIdType.MESH
PAD = 8
ROWS = 16


def kernel(
    chain,
    ticks,
    freqs,
    terms,
    labels,
    width,
    src_pos_in,
    wavelet_in,
    arriving,
    classes_in,
    filters_in,
    rec_pos_in,
    rec_data_in,
    image,
    passing,
    src_pos,
    wavelet,
    classes,
    filters,
    rec_pos,
    rec_data,
    fields,
    leaving,
    table,
    coef,
    terms_buf,
    corr,
    illum,
    running,
    landed,
    in_sem,
    small_sem,
    out_sem,
    send_sem,
    recv_sem,
    tot_send,
    tot_recv,
):
    position = lax.axis_index("depth")
    has_next = position < chain - 1
    following_slab = lax.rem(position + 1, chain)
    is_first = position == 0

    def load_copy(kind, freq):
        return pltpu.make_async_copy(
            arriving.at[0, kind, :, freq], fields.at[0, kind, :, freq], in_sem.at[kind, freq]
        )

    def send_copy(tick, kind, freq):
        return pltpu.make_async_remote_copy(
            src_ref=leaving.at[tick, kind, :, freq],
            dst_ref=fields.at[tick + 1, kind, :, freq],
            send_sem=send_sem.at[tick, kind, freq],
            recv_sem=recv_sem.at[tick, kind, freq],
            device_id={"depth": following_slab},
            device_id_type=MESH,
        )

    def out_copy(kind, freq):
        return pltpu.make_async_copy(
            leaving.at[ticks - 1, kind, :, freq],
            passing.at[0, kind, :, freq],
            out_sem.at[kind, freq],
        )

    stages = chain.bit_length() - 1

    def partner(stage):
        distance = 1 << stage
        upper = lax.rem(position // distance, 2)
        return position + distance - 2 * distance * upper

    def total_copy(stage):
        return pltpu.make_async_remote_copy(
            src_ref=running.at[stage],
            dst_ref=landed.at[stage],
            send_sem=tot_send.at[stage],
            recv_sem=tot_recv.at[stage],
            device_id={"depth": partner(stage)},
            device_id_type=MESH,
        )

    def exchange(stage):
        if stage > 0:
            total_copy(stage - 1).wait_recv()
            running[stage] = running[stage - 1] + landed[stage - 1]
        if stage < stages:
            total_copy(stage).start()

    pairs = (
        (filters_in, filters),
        (classes_in, classes),
        (src_pos_in, src_pos),
        (wavelet_in, wavelet),
        (rec_pos_in, rec_pos),
        (rec_data_in, rec_data),
    )
    small = [
        pltpu.make_async_copy(here, there, small_sem.at[i]) for i, (here, there) in enumerate(pairs)
    ]
    small[0].start()
    small[1].start()
    for kind in range(2):
        for freq in range(freqs):
            load_copy(kind, freq).start()

    barrier = pltpu.get_barrier_semaphore()

    greeted = [(partner(stage), None) for stage in range(stages)]
    odd = lax.rem(position, 2)
    greeted.append((position + 1, (odd == 1) & (position < chain - 1)))
    greeted.append((position - 1, (odd == 0) & (position > 0)))
    for other, condition in greeted:

        def greet(other=other):
            pl.semaphore_signal(barrier, inc=1, device_id={"depth": other}, device_id_type=MESH)

        if condition is None:
            greet()
        else:
            pl.when(condition)(greet)
    end = (position == 0) | (position == chain - 1)
    greetings = stages + 1 - end.astype(jnp.int32)
    for copy in small[2:]:
        copy.start()

    corr[...] = jnp.zeros_like(corr)
    illum[...] = jnp.zeros_like(illum)
    edge = jnp.zeros((2, terms, PAD, width), jnp.float32)
    terms_buf[:, :, 0:PAD, :] = edge
    terms_buf[:, :, PAD + width : 2 * PAD + width, :] = edge
    small[0].wait()
    groups = width // labels
    for group in range(filters.shape[0] // width):
        rows = filters[group * width : (group + 1) * width, :]
        rows = jnp.concatenate(
            [rows, jnp.zeros((width, width - rows.shape[1]), jnp.float32)], axis=1
        )
        blocks = jnp.transpose(rows)[: table.shape[1], :]
        for slot in range(groups):
            shifted = blocks if slot == 0 else pltpu.roll(blocks, width - slot * labels, 1)
            table[group * groups + slot] = shifted

    def gather_coefficients(tick, freq):
        block = tick - position + chain - 1
        rows = [
            jnp.broadcast_to(table[freq * (2 * terms) + item, pl.ds(block, 1), :], (8, width))
            for item in range(2 * terms)
        ]
        for tile in range(0, width, 8):
            cells = classes[0, tile : tile + 8, :]
            for item in range(2 * terms):
                coef[tick, freq, item // terms, item % terms, tile : tile + 8, :] = jnp.take_along_axis(
                    rows[item], cells, axis=1, mode="promise_in_bounds"
                )

    lane = lax.broadcasted_iota(jnp.int32, (ROWS, width), 1)
    first_lane = lane == 0
    last_lane = lane == width - 1

    def depth_step(tick, kind, freq):
        target = leaving.at[tick]
        tiles = range(0, width, ROWS)
        for part in range(2):
            for tile in tiles:
                terms_buf[part, 0, PAD + tile : PAD + tile + ROWS, :] = fields[
                    tick, kind, part, freq, tile : tile + ROWS, :
                ]
        for term in range(1, terms):
            for part in range(2):
                for tile in tiles:
                    low = PAD + tile
                    centre = terms_buf[part, term - 1, low : low + ROWS, :]
                    twice = centre + centre
                    rows = (
                        terms_buf[part, term - 1, low - 1 : low - 1 + ROWS, :]
                        + terms_buf[part, term - 1, low + 1 : low + 1 + ROWS, :]
                    ) + twice
                    left = jnp.where(first_lane, 0.0, pltpu.roll(rows, 1, 1))
                    right = jnp.where(last_lane, 0.0, pltpu.roll(rows, width - 1, 1))
                    total = (left + right) + (rows + rows)
                    if term == 1:
                        value = 0.125 * total - centre
                    else:
                        previous = terms_buf[part, term - 2, low : low + ROWS, :]
                        value = 0.25 * total - (twice + previous)
                    terms_buf[part, term, low : low + ROWS, :] = value
        for tile in tiles:
            cells = slice(tile, tile + ROWS)
            padded = slice(PAD + tile, PAD + tile + ROWS)
            real, imag = None, None
            for term in range(terms):
                c_real = coef[tick, freq, 0, term, cells, :]
                c_imag = coef[tick, freq, 1, term, cells, :]
                q_real = terms_buf[0, term, padded, :]
                q_imag = terms_buf[1, term, padded, :]
                if kind == 0:
                    new_real = c_real * q_real - c_imag * q_imag
                    new_imag = c_real * q_imag + c_imag * q_real
                else:
                    new_real = c_real * q_real + c_imag * q_imag
                    new_imag = c_real * q_imag - c_imag * q_real
                real = new_real if term == 0 else real + new_real
                imag = new_imag if term == 0 else imag + new_imag
            target[kind, 0, freq, cells, :] = real
            target[kind, 1, freq, cells, :] = imag
            field_real = fields[tick, 0, 0, freq, cells, :]
            field_imag = fields[tick, 0, 1, freq, cells, :]
            if kind == 0:
                illum[cells, :] += field_real * field_real + field_imag * field_imag
            else:
                corr[cells, :] += (
                    field_real * fields[tick, 1, 0, freq, cells, :]
                    + field_imag * fields[tick, 1, 1, freq, cells, :]
                )

    def inject_source(tick):
        if tick == 0:
            small[2].wait()
            small[3].wait()
        grid_x = lax.broadcasted_iota(jnp.int32, (width, width), 0)
        grid_y = lax.broadcasted_iota(jnp.int32, (width, width), 1)
        hits = [
            (grid_x == src_pos[tick, 0, e]) & (grid_y == src_pos[tick, 1, e])
            for e in range(src_pos.shape[2])
        ]
        for part in range(2):
            for freq in range(freqs):
                plane = jnp.zeros((width, width), jnp.float32)
                for e, hit in enumerate(hits):
                    plane = plane + jnp.where(hit, wavelet[tick, e, part, freq], 0.0)
                fields[tick + 1, 0, part, freq] = plane

    def inject_receiver(tick):
        if tick == 0:
            small[4].wait()
            small[5].wait()
        receivers = rec_pos.shape[1]
        cell = lax.broadcasted_iota(jnp.int32, (width, receivers), 0)
        hits_x = jnp.where(cell == rec_pos[0:1, :], 1.0, 0.0).astype(jnp.bfloat16)
        hits_y = jnp.where(cell == rec_pos[1:2, :], 1.0, 0.0).astype(jnp.bfloat16)
        for part in range(2):
            stacked = []
            for freq in range(freqs):
                weights = rec_data[tick, part, freq : freq + 1, :]
                for _ in range(3):
                    piece = weights.astype(jnp.bfloat16)
                    weights = weights - piece.astype(jnp.float32)
                    stacked.append(hits_x * piece)
            product = lax.dot_general(
                jnp.concatenate(stacked, axis=0),
                hits_y,
                (((1,), (1,)), ((), ())),
                preferred_element_type=jnp.float32,
            )
            for freq in range(freqs):
                low = 3 * freq * width
                fields[tick + 1, 1, part, freq] = (
                    product[low : low + width]
                    + product[low + width : low + 2 * width]
                    + product[low + 2 * width : low + 3 * width]
                )

    small[1].wait()
    for kind in range(2):
        for tick in range(ticks):
            if tick > 0:
                inject = inject_source if kind == 0 else inject_receiver
                pl.when(is_first)(functools.partial(inject, tick - 1))

            def chunk(freq, carry, tick=tick, kind=kind):
                if kind == 0:
                    gather_coefficients(tick, freq)
                if tick == 0:
                    load_copy(kind, freq).wait()
                else:

                    @pl.when(position > 0)
                    def _():
                        send_copy(tick - 1, kind, freq).wait_recv()

                depth_step(tick, kind, freq)
                if tick == 0 and kind == 0:

                    @pl.when(freq == 0)
                    def _():
                        pl.semaphore_wait(barrier, greetings)

                if tick < ticks - 1:

                    @pl.when(has_next)
                    def _():
                        send_copy(tick, kind, freq).start()
                else:
                    out_copy(kind, freq).start()
                for stage in range(1, stages + 1):
                    turn = 2 * stage - 1
                    if stage < stages and kind == 1 and tick == turn // freqs:
                        pl.when(freq == turn % freqs)(functools.partial(exchange, stage))
                return carry

            lax.fori_loop(0, freqs, chunk, 0)
            if kind == 0 and tick == ticks - 1:
                running[0] = jnp.sum(illum[...].reshape(width // 8, 8, width), axis=0)
                exchange(0)

    exchange(stages)
    energy = jnp.sum(running[stages], keepdims=True)
    damping = energy / (chain * width * width)
    image[0] = math.sqrt(ticks * freqs) * corr[...] / (illum[...] + damping)

    for stage in range(stages):
        total_copy(stage).wait_send()

    @pl.when(jnp.logical_not(is_first))
    def _():
        for copy in small[2:]:
            copy.wait()

    for kind in range(2):
        for freq in range(freqs):
            for tick in range(ticks - 1):

                @pl.when(has_next)
                def _():
                    send_copy(tick, kind, freq).wait_send()

            out_copy(kind, freq).wait()


def solution(mesh):
    chain = mesh.shape["depth"]

    def body(arriving, classes, filters, src_pos, wavelet, rec_pos, rec_data):
        _, kinds, parts, freqs, width, _ = arriving.shape
        ticks = wavelet.shape[0] + 1
        terms, labels = filters.shape[3:]
        blocks = filters.shape[0]
        columns = filters.transpose(1, 2, 3, 4, 0).reshape(-1, blocks)
        f32 = jnp.float32
        stages = chain.bit_length() - 1
        vmem = pl.BlockSpec(memory_space=pltpu.VMEM)
        hbm = pl.BlockSpec(memory_space=pltpu.HBM)
        window = (ticks, kinds, parts, freqs, width, width)
        return pl.pallas_call(
            functools.partial(kernel, chain, ticks, freqs, terms, labels, width),
            out_shape=(
                jax.ShapeDtypeStruct((1, width, width), f32),
                jax.ShapeDtypeStruct(arriving.shape, f32),
            ),
            in_specs=[hbm] * 7,
            out_specs=(vmem, hbm),
            scratch_shapes=[
                pltpu.SMEM(src_pos.transpose(0, 2, 1).shape, jnp.int32),
                pltpu.SMEM(wavelet.shape, f32),
                pltpu.VMEM(classes.shape, jnp.int32),
                pltpu.VMEM(columns.shape, f32),
                pltpu.VMEM(rec_pos.T.shape, jnp.int32),
                pltpu.VMEM(rec_data.shape, f32),
                pltpu.VMEM(window, f32),
                pltpu.VMEM(window, f32),
                pltpu.VMEM((freqs * parts * terms, pl.cdiv(blocks, 8) * 8, width), f32),
                pltpu.VMEM((ticks, freqs, parts, terms, width, width), f32),
                pltpu.VMEM((parts, terms, width + 2 * PAD, width), f32),
                pltpu.VMEM((width, width), f32),
                pltpu.VMEM((width, width), f32),
                pltpu.VMEM((stages + 1, 8, width), f32),
                pltpu.VMEM((stages, 8, width), f32),
                pltpu.SemaphoreType.DMA((kinds, freqs)),
                pltpu.SemaphoreType.DMA((6,)),
                pltpu.SemaphoreType.DMA((kinds, freqs)),
                pltpu.SemaphoreType.DMA((ticks - 1, kinds, freqs)),
                pltpu.SemaphoreType.DMA((ticks - 1, kinds, freqs)),
                pltpu.SemaphoreType.DMA((stages,)),
                pltpu.SemaphoreType.DMA((stages,)),
            ],
            compiler_params=pltpu.CompilerParams(
                collective_id=0, has_side_effects=True, vmem_limit_bytes=67043328 - 1200000
            ),
        )(src_pos.transpose(0, 2, 1), wavelet, arriving, classes, columns, rec_pos.T, rec_data)

    return jax.shard_map(
        body,
        mesh=mesh,
        in_specs=(
            P(("survey", "depth"), None, None, None, None, None),
            P("depth", None, None),
            P(),
            P("survey", None, None),
            P("survey", None, None, None),
            P("survey", None),
            P("survey", None, None, None),
        ),
        out_specs=(
            P(("survey", "depth"), None, None),
            P(("survey", "depth"), None, None, None, None, None),
        ),
        check_vma=False,
    )
```

```python
import functools
import math

import jax
import jax.numpy as jnp
from jax import lax
from jax.experimental import pallas as pl
from jax.experimental.pallas import tpu as pltpu
from jax.sharding import PartitionSpec as P

MESH = pl.DeviceIdType.MESH
PAD = 8
ROWS = 16


def kernel(
    chain,
    ticks,
    freqs,
    terms,
    labels,
    width,
    src_pos_in,
    wavelet_in,
    arriving,
    classes_in,
    filters_in,
    rec_pos_in,
    rec_data_in,
    image,
    passing,
    src_pos,
    wavelet,
    classes,
    filters,
    rec_pos,
    rec_data,
    fields,
    leaving,
    table,
    coef,
    terms_buf,
    corr,
    illum,
    running,
    landed,
    in_sem,
    small_sem,
    out_sem,
    send_sem,
    recv_sem,
    tot_send,
    tot_recv,
):
    position = lax.axis_index("depth")
    has_next = position < chain - 1
    following_slab = lax.rem(position + 1, chain)
    is_first = position == 0

    def load_copy(kind, freq):
        return pltpu.make_async_copy(
            arriving.at[0, kind, :, freq], fields.at[0, kind, :, freq], in_sem.at[kind, freq]
        )

    def send_copy(tick, kind, freq):
        return pltpu.make_async_remote_copy(
            src_ref=leaving.at[tick, kind, :, freq],
            dst_ref=fields.at[tick + 1, kind, :, freq],
            send_sem=send_sem.at[tick, kind, freq],
            recv_sem=recv_sem.at[tick, kind, freq],
            device_id={"depth": following_slab},
            device_id_type=MESH,
        )

    def out_copy(kind, freq):
        return pltpu.make_async_copy(
            leaving.at[ticks - 1, kind, :, freq],
            passing.at[0, kind, :, freq],
            out_sem.at[kind, freq],
        )

    stages = chain.bit_length() - 1

    def partner(stage):
        distance = 1 << stage
        upper = lax.rem(position // distance, 2)
        return position + distance - 2 * distance * upper

    def total_copy(stage):
        return pltpu.make_async_remote_copy(
            src_ref=running.at[stage],
            dst_ref=landed.at[stage],
            send_sem=tot_send.at[stage],
            recv_sem=tot_recv.at[stage],
            device_id={"depth": partner(stage)},
            device_id_type=MESH,
        )

    def exchange(stage):
        if stage > 0:
            total_copy(stage - 1).wait_recv()
            running[stage] = running[stage - 1] + landed[stage - 1]
        if stage < stages:
            total_copy(stage).start()

    pairs = (
        (filters_in, filters),
        (classes_in, classes),
        (src_pos_in, src_pos),
        (wavelet_in, wavelet),
        (rec_pos_in, rec_pos),
        (rec_data_in, rec_data),
    )
    small = [
        pltpu.make_async_copy(here, there, small_sem.at[i]) for i, (here, there) in enumerate(pairs)
    ]
    small[0].start()
    small[1].start()
    for kind in range(2):
        for freq in range(freqs):
            load_copy(kind, freq).start()

    barrier = pltpu.get_barrier_semaphore()

    greeted = [(partner(stage), None) for stage in range(stages)]
    odd = lax.rem(position, 2)
    greeted.append((position + 1, (odd == 1) & (position < chain - 1)))
    greeted.append((position - 1, (odd == 0) & (position > 0)))
    for other, condition in greeted:

        def greet(other=other):
            pl.semaphore_signal(barrier, inc=1, device_id={"depth": other}, device_id_type=MESH)

        if condition is None:
            greet()
        else:
            pl.when(condition)(greet)
    end = (position == 0) | (position == chain - 1)
    greetings = stages + 1 - end.astype(jnp.int32)
    for copy in small[2:]:
        copy.start()

    corr[...] = jnp.zeros_like(corr)
    illum[...] = jnp.zeros_like(illum)
    edge = jnp.zeros((2, terms, PAD, width), jnp.float32)
    terms_buf[:, :, 0:PAD, :] = edge
    terms_buf[:, :, PAD + width : 2 * PAD + width, :] = edge
    small[0].wait()
    groups = width // labels
    for group in range(filters.shape[0] // width):
        rows = filters[group * width : (group + 1) * width, :]
        rows = jnp.concatenate(
            [rows, jnp.zeros((width, width - rows.shape[1]), jnp.float32)], axis=1
        )
        blocks = jnp.transpose(rows)[: table.shape[1], :]
        for slot in range(groups):
            shifted = blocks if slot == 0 else pltpu.roll(blocks, width - slot * labels, 1)
            table[group * groups + slot] = shifted

    def gather_coefficients(tick, freq):
        block = tick - position + chain - 1
        rows = [
            jnp.broadcast_to(table[freq * (2 * terms) + item, pl.ds(block, 1), :], (8, width))
            for item in range(2 * terms)
        ]
        for tile in range(0, width, 8):
            cells = classes[0, tile : tile + 8, :]
            for item in range(2 * terms):
                coef[tick, freq, item // terms, item % terms, tile : tile + 8, :] = jnp.take_along_axis(
                    rows[item], cells, axis=1, mode="promise_in_bounds"
                )

    lane = lax.broadcasted_iota(jnp.int32, (ROWS, width), 1)
    first_lane = lane == 0
    last_lane = lane == width - 1

    def depth_step(tick, kind, freq):
        target = leaving.at[tick]
        tiles = range(0, width, ROWS)
        for part in range(2):
            for tile in tiles:
                terms_buf[part, 0, PAD + tile : PAD + tile + ROWS, :] = fields[
                    tick, kind, part, freq, tile : tile + ROWS, :
                ]
        for term in range(1, terms):
            for part in range(2):
                for tile in tiles:
                    low = PAD + tile
                    centre = terms_buf[part, term - 1, low : low + ROWS, :]
                    twice = centre + centre
                    rows = (
                        terms_buf[part, term - 1, low - 1 : low - 1 + ROWS, :]
                        + terms_buf[part, term - 1, low + 1 : low + 1 + ROWS, :]
                    ) + twice
                    left = jnp.where(first_lane, 0.0, pltpu.roll(rows, 1, 1))
                    right = jnp.where(last_lane, 0.0, pltpu.roll(rows, width - 1, 1))
                    total = (left + right) + (rows + rows)
                    if term == 1:
                        value = 0.125 * total - centre
                    else:
                        previous = terms_buf[part, term - 2, low : low + ROWS, :]
                        value = 0.25 * total - (twice + previous)
                    terms_buf[part, term, low : low + ROWS, :] = value
        for tile in tiles:
            cells = slice(tile, tile + ROWS)
            padded = slice(PAD + tile, PAD + tile + ROWS)
            real, imag = None, None
            for term in range(terms):
                c_real = coef[tick, freq, 0, term, cells, :]
                c_imag = coef[tick, freq, 1, term, cells, :]
                q_real = terms_buf[0, term, padded, :]
                q_imag = terms_buf[1, term, padded, :]
                if kind == 0:
                    new_real = c_real * q_real - c_imag * q_imag
                    new_imag = c_real * q_imag + c_imag * q_real
                else:
                    new_real = c_real * q_real + c_imag * q_imag
                    new_imag = c_real * q_imag - c_imag * q_real
                real = new_real if term == 0 else real + new_real
                imag = new_imag if term == 0 else imag + new_imag
            target[kind, 0, freq, cells, :] = real
            target[kind, 1, freq, cells, :] = imag
            field_real = fields[tick, 0, 0, freq, cells, :]
            field_imag = fields[tick, 0, 1, freq, cells, :]
            if kind == 0:
                illum[cells, :] += field_real * field_real + field_imag * field_imag
            else:
                corr[cells, :] += (
                    field_real * fields[tick, 1, 0, freq, cells, :]
                    + field_imag * fields[tick, 1, 1, freq, cells, :]
                )

    def inject_source(tick):
        if tick == 0:
            small[2].wait()
            small[3].wait()
        grid_x = lax.broadcasted_iota(jnp.int32, (width, width), 0)
        grid_y = lax.broadcasted_iota(jnp.int32, (width, width), 1)
        hits = [
            (grid_x == src_pos[tick, 0, e]) & (grid_y == src_pos[tick, 1, e])
            for e in range(src_pos.shape[2])
        ]
        for part in range(2):
            for freq in range(freqs):
                plane = jnp.zeros((width, width), jnp.float32)
                for e, hit in enumerate(hits):
                    plane = plane + jnp.where(hit, wavelet[tick, e, part, freq], 0.0)
                fields[tick + 1, 0, part, freq] = plane

    def inject_receiver(tick):
        if tick == 0:
            small[4].wait()
            small[5].wait()
        receivers = rec_pos.shape[1]
        cell = lax.broadcasted_iota(jnp.int32, (width, receivers), 0)
        hits_x = jnp.where(cell == rec_pos[0:1, :], 1.0, 0.0).astype(jnp.bfloat16)
        hits_y = jnp.where(cell == rec_pos[1:2, :], 1.0, 0.0).astype(jnp.bfloat16)
        for part in range(2):
            stacked = []
            for freq in range(freqs):
                weights = rec_data[tick, part, freq : freq + 1, :]
                for _ in range(3):
                    piece = weights.astype(jnp.bfloat16)
                    weights = weights - piece.astype(jnp.float32)
                    stacked.append(hits_x * piece)
            product = lax.dot_general(
                jnp.concatenate(stacked, axis=0),
                hits_y,
                (((1,), (1,)), ((), ())),
                preferred_element_type=jnp.float32,
            )
            for freq in range(freqs):
                low = 3 * freq * width
                fields[tick + 1, 1, part, freq] = (
                    product[low : low + width]
                    + product[low + width : low + 2 * width]
                    + product[low + 2 * width : low + 3 * width]
                )

    small[1].wait()
    for kind in range(2):
        for tick in range(ticks):
            if tick > 0:
                inject = inject_source if kind == 0 else inject_receiver
                pl.when(is_first)(functools.partial(inject, tick - 1))

            def chunk(freq, carry, tick=tick, kind=kind):
                if kind == 0:
                    gather_coefficients(tick, freq)
                if tick == 0:
                    load_copy(kind, freq).wait()
                else:

                    @pl.when(position > 0)
                    def _():
                        send_copy(tick - 1, kind, freq).wait_recv()

                depth_step(tick, kind, freq)
                if tick == 0 and kind == 0:

                    @pl.when(freq == 0)
                    def _():
                        pl.semaphore_wait(barrier, greetings)

                if tick < ticks - 1:

                    @pl.when(has_next)
                    def _():
                        send_copy(tick, kind, freq).start()
                else:
                    out_copy(kind, freq).start()
                for stage in range(1, stages + 1):
                    turn = 2 * stage - 1
                    if stage < stages and kind == 1 and tick == turn // freqs:
                        pl.when(freq == turn % freqs)(functools.partial(exchange, stage))
                return carry

            lax.fori_loop(0, freqs, chunk, 0)
            if kind == 0 and tick == ticks - 1:
                running[0] = jnp.sum(illum[...].reshape(width // 8, 8, width), axis=0)
                exchange(0)

    exchange(stages)
    energy = jnp.sum(running[stages], keepdims=True)
    damping = energy / (chain * width * width)
    image[0] = math.sqrt(ticks * freqs) * corr[...] / (illum[...] + damping)

    for stage in range(stages):
        total_copy(stage).wait_send()

    @pl.when(jnp.logical_not(is_first))
    def _():
        for copy in small[2:]:
            copy.wait()

    for kind in range(2):
        for freq in range(freqs):
            for tick in range(ticks - 1):

                @pl.when(has_next)
                def _():
                    send_copy(tick, kind, freq).wait_send()

            out_copy(kind, freq).wait()


def solution(mesh):
    chain = mesh.shape["depth"]

    def body(arriving, classes, filters, src_pos, wavelet, rec_pos, rec_data):
        _, kinds, parts, freqs, width, _ = arriving.shape
        ticks = wavelet.shape[0] + 1
        terms, labels = filters.shape[3:]
        blocks = filters.shape[0]
        columns = filters.transpose(1, 2, 3, 4, 0).reshape(-1, blocks)
        f32 = jnp.float32
        stages = chain.bit_length() - 1
        vmem = pl.BlockSpec(memory_space=pltpu.VMEM)
        hbm = pl.BlockSpec(memory_space=pltpu.HBM)
        window = (ticks, kinds, parts, freqs, width, width)
        return pl.pallas_call(
            functools.partial(kernel, chain, ticks, freqs, terms, labels, width),
            out_shape=(
                jax.ShapeDtypeStruct((1, width, width), f32),
                jax.ShapeDtypeStruct(arriving.shape, f32),
            ),
            in_specs=[hbm] * 7,
            out_specs=(vmem, hbm),
            scratch_shapes=[
                pltpu.SMEM(src_pos.transpose(0, 2, 1).shape, jnp.int32),
                pltpu.SMEM(wavelet.shape, f32),
                pltpu.VMEM(classes.shape, jnp.int32),
                pltpu.VMEM(columns.shape, f32),
                pltpu.VMEM(rec_pos.T.shape, jnp.int32),
                pltpu.VMEM(rec_data.shape, f32),
                pltpu.VMEM(window, f32),
                pltpu.VMEM(window, f32),
                pltpu.VMEM((freqs * parts * terms, pl.cdiv(blocks, 8) * 8, width), f32),
                pltpu.VMEM((ticks, freqs, parts, terms, width, width), f32),
                pltpu.VMEM((parts, terms, width + 2 * PAD, width), f32),
                pltpu.VMEM((width, width), f32),
                pltpu.VMEM((width, width), f32),
                pltpu.VMEM((stages + 1, 8, width), f32),
                pltpu.VMEM((stages, 8, width), f32),
                pltpu.SemaphoreType.DMA((kinds, freqs)),
                pltpu.SemaphoreType.DMA((6,)),
                pltpu.SemaphoreType.DMA((kinds, freqs)),
                pltpu.SemaphoreType.DMA((ticks - 1, kinds, freqs)),
                pltpu.SemaphoreType.DMA((ticks - 1, kinds, freqs)),
                pltpu.SemaphoreType.DMA((stages,)),
                pltpu.SemaphoreType.DMA((stages,)),
            ],
            compiler_params=pltpu.CompilerParams(
                collective_id=0, has_side_effects=True, vmem_limit_bytes=67043328 - 20000000
            ),
        )(
            *(
                pltpu.with_memory_space_constraint(operand, pltpu.HBM)
                for operand in (
                    src_pos.transpose(0, 2, 1),
                    wavelet,
                    arriving,
                    classes,
                    columns,
                    rec_pos.T,
                    rec_data,
                )
            )
        )

    return jax.shard_map(
        body,
        mesh=mesh,
        in_specs=(
            P(("survey", "depth"), None, None, None, None, None),
            P("depth", None, None),
            P(),
            P("survey", None, None),
            P("survey", None, None, None),
            P("survey", None),
            P("survey", None, None, None),
        ),
        out_specs=(
            P(("survey", "depth"), None, None),
            P(("survey", "depth"), None, None, None, None, None),
        ),
        check_vma=False,
    )
```
